256 devices in a mesh: row: 16 (over y_lo, z), col: 16 (over y_hi, x, core).
Axes of the slice: x: 4, y: 4 (y_hi: 2, y_lo: 2; y = y_hi * 2 + y_lo), z: 8, core: 2. Of those that a mesh axis runs over, the one named last changes fastest.
Arguments:
- env: float32 [1024, 32768], P('row', 'col'), may hold values from -0.03125 to 0.03125
- wave: float32 [32768, 2048], P('row', 'col'), may hold values from -6 to 6
- mpo: float32 [16, 16], replicated, may hold values from -1.5 to 1.5
Outputs:
- applied: float32 [1024, 2048], P('row', 'col')
The draws below stay inside these ranges and needn't reach their ends.
All inputs are finite; a program needn't handle non-finite values.
Results may differ from the reference program's by a relative error of at most 0.00007.
Values sent between devices are 32-bit elements; how exact they have to be, the bound alone decides.
A program may use at most 128 MiB of HBM per device.

```python
import jax
import jax.numpy as jnp
from jax import lax

L = 32768
S = 16
ROWS = 1024
R = 128


def levels(stream_key, shape, shards, least, high):
    loudness = 1.0
    for position, blocks in shards:
        heights = jax.random.uniform(jax.random.fold_in(jax.random.fold_in(stream_key, 6), position), (blocks,), jnp.float32, least / len(shards), high / len(shards))
        loudness = loudness * jnp.repeat(jnp.exp(heights), shape[position] // blocks).reshape((-1,) + (1,) * (len(shape) - 1 - position))
    return loudness


def gaussian(rng, shape, scale, most, pieces=(), kind=jnp.bfloat16):
    factor_of = levels(rng, shape, pieces, -0.22, 0.18) if pieces else 1.0
    values = jax.random.normal(rng, shape, jnp.float32) * scale * factor_of
    return jnp.minimum(jnp.maximum(values, -most), most).astype(kind)


def setup_inputs(seed: int = 0) -> dict:
    key_of = jax.random.split(jax.random.key(seed), 4)
    env = gaussian(key_of[0], (ROWS, L), L ** -0.5, 0.03125, ((0, 16), (1, 16)), jnp.float32)
    wave = gaussian(key_of[1], (L, R * S), 1.0, 6.0, ((0, 16), (1, 16)), jnp.float32)
    mpo = gaussian(key_of[2], (S, S), S ** -0.5, 1.5, (), jnp.float32)
    return dict(env=env, wave=wave, mpo=mpo)


def reference(env, wave, mpo):
    spins = mpo.shape[0]
    left = wave.shape[0]
    right = wave.shape[1] // spins
    wave3 = wave.reshape(left, right, spins)
    mixed = jnp.einsum("krs,st->ktr", wave3, mpo, precision=lax.Precision.HIGHEST)
    flat = mixed.reshape(left, spins * right)
    return jnp.dot(env, flat, precision=lax.Precision.HIGHEST, preferred_element_type=jnp.float32)
```

```python
import jax
import jax.numpy as jnp
from jax import lax
from jax.sharding import PartitionSpec as P


def shards(env, wave, mpo):
    n = lax.axis_size("row")
    spins = mpo.shape[0]
    swap = [(a * n + b, b * n + a) for a in range(n) for b in range(n)]
    moved = lax.ppermute(env, ("row", "col"), swap)
    env_k = lax.all_gather(moved, "col", axis=0, tiled=True)
    part = jnp.dot(env_k, wave, precision=lax.Precision.HIGHEST, preferred_element_type=jnp.float32)
    block = lax.psum_scatter(part, "row", scatter_dimension=0, tiled=True)
    rows = block.shape[0]
    mixed = jnp.einsum("irs,st->tir", block.reshape(rows, -1, spins), mpo, precision=lax.Precision.HIGHEST)
    spun = lax.all_to_all(mixed, "col", split_axis=0, concat_axis=2, tiled=True)
    return spun.reshape(rows, -1)


def solution(mesh):
    in_specs = (P("row", "col"), P("row", "col"), P())
    out_specs = P("row", "col")
    return jax.shard_map(shards, mesh=mesh, in_specs=in_specs, out_specs=out_specs, check_vma=False)
```

```python
import functools

import jax
import jax.numpy as jnp
from jax import lax
from jax.experimental import pallas as pl
from jax.experimental.pallas import tpu as pltpu
from jax.sharding import PartitionSpec as P

MESH = pl.DeviceIdType.MESH
CHUNKS = 4
X, Z = 4, 8


def device(yh, yl, x, z, core):
    return (yl * Z + z, yh * 2 * X + x * 2 + core)


def split(value):
    high = value.astype(jnp.bfloat16)
    return high, (value - high.astype(jnp.float32)).astype(jnp.bfloat16)


def dot(a, b):
    return jnp.dot(a, b, preferred_element_type=jnp.float32)


def kernel(
    env, wave, mpo, out, spread, gathered, waves, wave_high, wave_low, part, other, summed, landed, mixed, final,
    a_send, a_recv, b_send, b_recv, w_send, w_recv, w_local, g_send, g_recv, c_send, c_recv,
    y_send, y_recv, z_send, z_recv, f_send, f_recv,
):
    row, col = lax.axis_index("row"), lax.axis_index("col")
    yl, z = row // Z, row % Z
    yh, x, core = col // (2 * X), (col // 2) % X, col % 2
    chunks, n, height, _ = summed.shape

    def remote(src, dst, send, recv, to):
        return pltpu.make_async_remote_copy(
            src_ref=src, dst_ref=dst, send_sem=send, recv_sem=recv, device_id=to, device_id_type=MESH
        )

    def wait(ref, sem):
        pltpu.make_async_copy(ref, ref, sem).wait()

    right = device(yh, yl, (x + 1) % X, z, core)
    left = device(yh, yl, (x + X - 1) % X, z, core)
    sibling = device(yh, yl, x, z, 1 - core)
    across = device(1 - yh, yl, x, z, core)

    barrier = pltpu.get_barrier_semaphore()

    def greet(to):
        pl.semaphore_signal(barrier, inc=1, device_id=to, device_id_type=MESH)

    for step in range(1, X):
        greet(device(yh, yl, (x + step) % X, z, core))
    greet(sibling)
    greet(across)
    source = yl * 2 * X + x * 2 + z % 2

    @pl.loop(0, n)
    def _(j):
        greet((j, source))

    @pl.loop(1, n)
    def _(j):
        greet(((row + j) % n, col))
        greet((row, (col + j) % n))

    own_wave = pltpu.make_async_copy(wave.at[:, yh], waves.at[yh], w_local)
    own_wave.start()

    spins = mpo.shape[0]
    size = mixed.shape[0] * mixed.shape[1]
    rights = size // spins
    wide = lax.broadcasted_iota(jnp.int32, (size, spins), 0)
    pick_t = (wide // rights == lax.broadcasted_iota(jnp.int32, (size, spins), 1)).astype(jnp.float32)
    tall = lax.broadcasted_iota(jnp.int32, (spins, size), 1)
    pick_s = (tall % spins == lax.broadcasted_iota(jnp.int32, (spins, size), 0)).astype(jnp.float32)
    by_t = lax.dot_general(
        pick_t, mpo[...], (((1,), (1,)), ((), ())), precision=lax.Precision.HIGHEST,
        preferred_element_type=jnp.float32,
    )
    full = jnp.dot(by_t, pick_s, precision=lax.Precision.HIGHEST, preferred_element_type=jnp.float32)
    same = (
        lax.broadcasted_iota(jnp.int32, (size, size), 0) % rights
        == lax.broadcasted_iota(jnp.int32, (size, size), 1) // spins
    )
    mixing = jnp.where(same, full, 0.0)

    pl.semaphore_wait(barrier, (X - 1) + 2 + n + 2 * (n - 1))

    wide_k = spread.shape[3]

    def slices(h, to_x):
        return env.at[pl.ds(h * height, height), pl.ds(pl.multiple_of(to_x * wide_k, wide_k), wide_k)]

    for h in range(chunks):
        for step in range(1, X):
            to_x = (x + step) % X
            remote(
                slices(h, to_x), spread.at[h, x], a_send.at[h], a_recv.at[h], device(yh, yl, to_x, z, core)
            ).start()
        pltpu.make_async_copy(slices(h, x), spread.at[h, x], a_recv.at[h]).start()
    crossing = remote(wave.at[:, 1 - yh], waves.at[yh], w_send, w_recv, across)
    crossing.start()

    has_self = (yl == yh) & (z % 2 == core)

    def forward(h):
        wait(spread.at[h], a_recv.at[h])

        @pl.loop(0, n)
        def _(i):
            j = (i + row) % n
            from_x, to_yh, to_core = j // 4, (j // 2) % 2, j % 2
            src = spread.at[h, from_x, :, pl.ds(pl.multiple_of((j % 4) * 128, 128), 128)]
            dst = gathered.at[h, 2 * x + to_core, row]
            to = device(to_yh, yh, x, 2 * from_x + core, to_core)
            here = has_self & (to_yh == yh) & (2 * from_x + core == z) & (to_core == core)

            @pl.when(jnp.logical_not(here))
            def _():
                remote(src, dst, b_send.at[h], b_recv.at[h], to).start()

            @pl.when(here)
            def _():
                pltpu.make_async_copy(src, dst, b_recv.at[h]).start()

    mine, from_left, from_right, far = (2 * ((x + s) % X) + core for s in (0, 3, 1, 2))
    half = n // 2

    def gather_own(h):
        wait(gathered.at[h, mine], b_recv.at[h])
        own = gathered.at[h, mine]
        remote(own, own, g_send.at[h, 0], g_recv.at[h, 0], right).start()
        remote(own, own, g_send.at[h, 1], g_recv.at[h, 1], left).start()
        remote(own, own, c_send.at[h, 0], c_recv.at[h, 0], sibling).start()

    def gather_relay(h):
        got = gathered.at[h, from_left]
        wait(got, g_recv.at[h, 0])
        low = gathered.at[h, from_left, pl.ds(0, half)]
        remote(low, low, g_send.at[h, 2], g_recv.at[h, 2], right).start()
        remote(got, got, c_send.at[h, 1], c_recv.at[h, 1], sibling).start()
        got = gathered.at[h, from_right]
        wait(got, g_recv.at[h, 1])
        high = gathered.at[h, from_right, pl.ds(half, half)]
        remote(high, high, g_send.at[h, 3], g_recv.at[h, 3], left).start()
        remote(got, got, c_send.at[h, 2], c_recv.at[h, 2], sibling).start()

    def gather_end(h):
        wait(gathered.at[h, far, pl.ds(0, half)], g_recv.at[h, 2])
        wait(gathered.at[h, far, pl.ds(half, half)], g_recv.at[h, 3])
        got = gathered.at[h, far]
        remote(got, got, c_send.at[h, 3], c_recv.at[h, 3], sibling).start()

    def wave_ready():
        own_wave.wait()
        crossing.wait_recv()
        for p in range(X):
            high, low = split(jnp.concatenate([waves[0, p], waves[1, p]], axis=1))
            wave_high[p] = high
            wave_low[p] = low

    def multiply(h):
        for s in range(4):
            wait(gathered.at[h, s], c_recv.at[h, s])
        total = None
        for p in range(X):
            block = jnp.concatenate(
                [gathered[h, 2 * p].reshape(n * height, 128), gathered[h, 2 * p + 1].reshape(n * height, 128)], axis=1
            )
            high, low = split(block)
            term = dot(high, wave_high[p]) + dot(high, wave_low[p]) + dot(low, wave_high[p])
            total = term if total is None else total + term
        part[h, 0] = total[:, :128].reshape(n, height, 128)
        part[h, 1] = total[:, 128:].reshape(n, height, 128)
        remote(part.at[h, 1 - yh], other.at[h], y_send.at[h], y_recv.at[h], across).start()

    def reduce(h):
        wait(other.at[h], y_recv.at[h])
        summed[h] = part[h, yh] + other[h]

        @pl.loop(1, n)
        def _(j):
            to = (row + j) % n
            remote(summed.at[h, to], landed.at[h, j - 1], z_send.at[h], z_recv.at[h], (to, col)).start()

    stages = (gather_own, gather_relay, gather_end, multiply, reduce)
    for h in range(chunks):
        forward(h)
    for step in range(chunks + len(stages) - 1):
        for s, stage in enumerate(stages):
            h = step - s
            if 0 <= h < chunks:
                if stage is multiply and h == 0:
                    wave_ready()
                stage(h)

    rows = []
    for h in range(chunks):
        wait(landed.at[h], z_recv.at[h])
        rows.append(summed[h, row] + jnp.sum(landed[h], axis=0))
    block = jnp.concatenate(rows + [jnp.zeros((128 - chunks * height, 128), jnp.float32)], axis=0)
    turned = lax.dot_general(
        mixing, block, (((1,), (1,)), ((), ())), precision=lax.Precision.HIGHEST, preferred_element_type=jnp.float32
    )
    mixed[...] = turned.reshape(mixed.shape)

    @pl.loop(1, n)
    def _(j):
        to = (col + j) % n
        remote(mixed.at[to], final.at[col], f_send, f_recv, (row, to)).start()

    final[col] = mixed[col]
    wait(final.at[pl.ds(0, n - 1)], f_recv)
    out[...] = final[...].reshape(size, 128).T[: chunks * height]

    wait(final.at[pl.ds(0, n - 1)], f_send)
    crossing.wait_send()
    for h in range(chunks):
        wait(spread.at[h, pl.ds(0, X - 1)], a_send.at[h])

        @pl.when(has_self)
        def _():
            wait(gathered.at[h, 0, pl.ds(0, n - 1)], b_send.at[h])

        @pl.when(jnp.logical_not(has_self))
        def _():
            wait(gathered.at[h, 0], b_send.at[h])

        for s in range(2):
            wait(gathered.at[h, 0], g_send.at[h, s])
            wait(gathered.at[h, 0, pl.ds(0, half)], g_send.at[h, 2 + s])
        for s in range(4):
            wait(gathered.at[h, 0], c_send.at[h, s])
        wait(other.at[h], y_send.at[h])
        wait(landed.at[h], z_send.at[h])


def shards(env, wave, mpo):
    n = lax.axis_size("row")
    rows, depth = env.shape
    height = rows // CHUNKS
    wave4 = wave.reshape(X, 2, depth // (2 * X), wave.shape[1])
    f32, bf16 = jnp.float32, jnp.bfloat16
    dma = pltpu.SemaphoreType.DMA
    h = CHUNKS
    return pl.pallas_call(
        kernel,
        out_shape=jax.ShapeDtypeStruct((rows, 128), f32),
        in_specs=[
            pl.BlockSpec(memory_space=pl.ANY),
            pl.BlockSpec(memory_space=pl.ANY),
            pl.BlockSpec(memory_space=pltpu.VMEM),
        ],
        out_specs=pl.BlockSpec(memory_space=pltpu.VMEM),
        scratch_shapes=[
            pltpu.VMEM((h, X, height, depth // X), f32),
            pltpu.VMEM((h, 2 * X, n, height, 128), f32),
            pltpu.VMEM((2, X, depth // (2 * X), 128), f32),
            pltpu.VMEM((X, depth // (2 * X), 256), bf16),
            pltpu.VMEM((X, depth // (2 * X), 256), bf16),
            pltpu.VMEM((h, 2, n, height, 128), f32),
            pltpu.VMEM((h, n, height, 128), f32),
            pltpu.VMEM((h, n, height, 128), f32),
            pltpu.VMEM((h, n - 1, height, 128), f32),
            pltpu.VMEM((n, 8, 128), f32),
            pltpu.VMEM((n, 8, 128), f32),
            dma((h,)), dma((h,)), dma((h,)), dma((h,)), dma, dma, dma, dma((h, 4)), dma((h, 4)), dma((h, 4)), dma((h, 4)),
            dma((h,)), dma((h,)), dma((h,)), dma((h,)), dma, dma,
        ],
        compiler_params=pltpu.CompilerParams(
            collective_id=0, has_side_effects=True, vmem_limit_bytes=40 * 1024 * 1024
        ),
    )(env, wave4, mpo)


def solution(mesh):
    in_specs = (P("row", "col"), P("row", "col"), P())
    out_specs = P("row", "col")
    return jax.shard_map(shards, mesh=mesh, in_specs=in_specs, out_specs=out_specs, check_vma=False)
```

```python
import functools

import jax
import jax.numpy as jnp
from jax import lax
from jax.experimental import pallas as pl
from jax.experimental.pallas import tpu as pltpu
from jax.sharding import PartitionSpec as P

MESH = pl.DeviceIdType.MESH
CHUNKS = 4
DIRECT = True
TRUNC = False
GATE_A = True
GATE_B = True
GATE_O = True
ORDER = (
    "A0", "W0", "W1", "W2", "W3", "S0", "A1", "B0", "A2",
    "A3", "B1", "O0", "B2", "O1", "B3", "S1", "V0", "O2",
    "M0", "O3", "M1", "R0", "M2", "R1", "M3", "R2", "R3",
)
X, Z = 4, 8


def device(yh, yl, x, z, core):
    return (yl * Z + z, yh * 2 * X + x * 2 + core)


def split(value):
    high = value.astype(jnp.bfloat16)
    return high, (value - high.astype(jnp.float32)).astype(jnp.bfloat16)


def dot(a, b):
    return jnp.dot(a, b, preferred_element_type=jnp.float32)


def kernel(
    env, wave, mpo, out, spread, gathered, waves, wave_high, wave_low, part, other, summed, landed, mixed, final, table,
    a_send, a_recv, b_send, b_recv, w_send, w_recv, s_send, s_recv, g_send, g_recv, y_send, y_recv, z_send, z_recv,
    f_send, f_recv, w_local, t_local,
):
    row, col = lax.axis_index("row"), lax.axis_index("col")
    yl, z = row // Z, row % Z
    yh, x, core = col // (2 * X), (col // 2) % X, col % 2
    chunks, n, height, _ = landed.shape

    def remote(src, dst, send, recv, to):
        return pltpu.make_async_remote_copy(
            src_ref=src, dst_ref=dst, send_sem=send, recv_sem=recv, device_id=to, device_id_type=MESH
        )

    def wait(ref, sem):
        pltpu.make_async_copy(ref, ref, sem).wait()

    right = device(yh, yl, (x + 1) % X, z, core)
    left = device(yh, yl, (x + X - 1) % X, z, core)
    opposite = device(yh, yl, (x + 2) % X, z, core)
    sibling = device(yh, yl, x, z, 1 - core)
    across = device(1 - yh, yl, x, z, core)

    barrier = pltpu.get_barrier_semaphore()

    def greet(to):
        pl.semaphore_signal(barrier, inc=1, device_id=to, device_id_type=MESH)

    for step in range(1, X):
        greet(device(yh, yl, (x + step) % X, z, core))
    greet(sibling)
    greet(across)
    source = yl * 2 * X + x * 2 + z % 2
    reducer = yh * 2 * X + x * 2 + row % 2

    @pl.loop(0, n // 2)
    def _(j):
        greet((2 * j + core, source))

    @pl.loop(0, n)
    def _(j):
        greet((j, reducer))

    @pl.loop(1, n)
    def _(j):
        greet((row, (col + j) % n))

    own_table = pltpu.make_async_copy(mpo, table, t_local)
    own_table.start()
    own_wave = pltpu.make_async_copy(wave.at[:, yh], waves.at[yh, core], w_local)
    own_wave.start()

    own_table.wait()
    spins = mpo.shape[0]
    size = mixed.shape[0] * mixed.shape[1]
    rights = size // spins
    wide = lax.broadcasted_iota(jnp.int32, (size, spins), 0)
    pick_t = (wide // rights == lax.broadcasted_iota(jnp.int32, (size, spins), 1)).astype(jnp.float32)
    tall = lax.broadcasted_iota(jnp.int32, (spins, size), 1)
    pick_s = (tall % spins == lax.broadcasted_iota(jnp.int32, (spins, size), 0)).astype(jnp.float32)
    by_t = lax.dot_general(
        pick_t, table[...], (((1,), (1,)), ((), ())), precision=lax.Precision.HIGHEST,
        preferred_element_type=jnp.float32,
    )
    full = jnp.dot(by_t, pick_s, precision=lax.Precision.HIGHEST, preferred_element_type=jnp.float32)
    same = (
        lax.broadcasted_iota(jnp.int32, (size, size), 0) % rights
        == lax.broadcasted_iota(jnp.int32, (size, size), 1) // spins
    )
    mixing = jnp.where(same, full, 0.0)

    pl.semaphore_wait(barrier, (X - 1) + 2 + n // 2 + n + (n - 1))

    wide_k = spread.shape[3]

    def slices(h, to_x):
        return env.at[pl.ds(h * height, height), pl.ds(pl.multiple_of(to_x * wide_k, wide_k), wide_k)]

    owed = {}

    def settle(*keys):
        for key in keys:
            if key in owed:
                owed.pop(key)()

    def start(key, src, dst, send, recv, to, landing=None):
        remote(src, dst, send, recv, to).start()
        owed[("sent", *key)] = lambda: wait(src, send)
        owed[("got", *key)] = lambda: wait(dst if landing is None else landing, recv)

    def spread_out(h):
        if GATE_A:
            settle(("sent", "a", h - 1))
        for step in range(1, X):
            to_x = (x + step) % X
            to = device(yh, yl, to_x, z, core)
            remote(slices(h, to_x), spread.at[h, x], a_send.at[h], a_recv.at[h], to).start()
        pltpu.make_async_copy(slices(h, x), spread.at[h, x], a_recv.at[h]).start()
        owed["sent", "a", h] = lambda: wait(spread.at[h, pl.ds(0, X - 1)], a_send.at[h])
        owed["got", "a", h] = lambda: wait(spread.at[h], a_recv.at[h])

    def cross(p):
        dst = waves.at[yh, core, p]
        start(("w", p), wave.at[p, 1 - yh], dst, w_send.at[p], w_recv.at[p], across, waves.at[1 - yh, core, p])

    def share(i):
        if i == 0:
            src = wave.at[:, yh]
        else:
            src = waves.at[1 - yh, core]
            settle(*(("got", "w", p) for p in range(X)))
        q = yh if i == 0 else 1 - yh
        start(("s", i), src, waves.at[q, core], s_send.at[i], s_recv.at[i], sibling, waves.at[q, 1 - core])

    def wave_ready(_):
        own_wave.wait()
        settle(("got", "s", 0), ("got", "s", 1))
        for p in range(X):
            high, low = split(jnp.concatenate([waves[q // 2, q % 2, p] for q in range(4)], axis=1))
            wave_high[p] = high
            wave_low[p] = low

    def scatter(key, count, piece, send, recv, whole, may_be_here):
        @pl.loop(0, count)
        def _(i):
            src, dst, to, here = piece(i)

            @pl.when(jnp.logical_not(here))
            def _():
                remote(src, dst, send, recv, to).start()

            @pl.when(here)
            def _():
                pltpu.make_async_copy(src, dst, recv).start()

        def sent():
            @pl.when(may_be_here)
            def _():
                wait(whole.at[pl.ds(0, count - 1)], send)

            @pl.when(jnp.logical_not(may_be_here))
            def _():
                wait(whole, send)

        owed[("sent", *key)] = sent
        owed[("got", *key)] = lambda: wait(whole, recv)

    def forward(h):
        settle(("got", "a", h))
        if GATE_B:
            settle(("sent", "b", h - 1))

        def piece(i):
            j = (i + row // 2) % (2 * X)
            from_x, to_yh = j // 2, j % 2
            src = spread.at[h, from_x, :, pl.ds(pl.multiple_of(to_yh * 256, 256), 256)]
            to = device(to_yh, yh, x, 2 * from_x + core, z % 2)
            here = (yl == yh) & (to_yh == yh) & (2 * from_x + core == z)
            return src, gathered.at[h, x, row // 2], to, here

        scatter(("b", h), 2 * X, piece, b_send.at[h], b_recv.at[h], gathered.at[h, x], (yl == yh) & (z % 2 == core))

    from_left, from_right, far = ((x + s) % X for s in (3, 1, 2))
    half = n // 4

    def gather_own(h):
        settle(("got", "b", h))
        if GATE_O:
            settle(("sent", "g", h - 1, 0), ("sent", "g", h - 1, 1))
        own = gathered.at[h, x]
        start(("g", h, 0), own, own, g_send.at[h, 0], g_recv.at[h, 0], right, gathered.at[h, from_left])
        start(("g", h, 1), own, own, g_send.at[h, 1], g_recv.at[h, 1], left, gathered.at[h, from_right])
        if DIRECT:
            start(("g", h, 2), own, own, g_send.at[h, 2], g_recv.at[h, 2], opposite, gathered.at[h, far])

    def gather_relay(h):
        for i, slot, to, first in ((0, from_left, right, 0), (1, from_right, left, half)):
            settle(("got", "g", h, i))
            piece = gathered.at[h, slot, pl.ds(first, half)]
            landing = gathered.at[h, far, pl.ds(first, half)]
            start(("g", h, 2 + i), piece, piece, g_send.at[h, 2 + i], g_recv.at[h, 2 + i], to, landing)

    def multiply(h):
        settle(*(("got", "g", h, i) for i in range(4)))
        total = None
        size = n // 2 * height
        for p in range(X):
            high, low = split(gathered[h, p].reshape(size, 256))
            both = dot(jnp.concatenate([high, low], axis=0), wave_high[p])
            term = both[:size] + both[size:] + dot(high, wave_low[p])
            total = term if total is None else total + term
        for q in range(4):
            part[h, q // 2, q % 2] = total[:, q * 128 : (q + 1) * 128].reshape(n // 2, height, 128)
        start(("y", h), part.at[h, 1 - yh], other.at[h], y_send.at[h], y_recv.at[h], across)

    def reduce(h):
        settle(("got", "y", h))
        summed[h] = part[h, yh] + other[h]

        def piece(i):
            j = (i + row) % n
            to = 2 * (j // 2) + core
            here = (to == row) & (j % 2 == core)
            src = summed.at[h, j % 2, j // 2]
            return src, landed.at[h, row], (to, yh * 2 * X + x * 2 + j % 2), here

        scatter(("z", h), n, piece, z_send.at[h], z_recv.at[h], landed.at[h], row % 2 == core)

    steps = dict(A=spread_out, B=forward, O=gather_own, L=gather_relay, M=multiply, R=reduce, W=cross, S=share, V=wave_ready)
    for step in ORDER:
        steps[step[0]](int(step[1:]))

    if TRUNC:
        out[...] = mixing[:64]
        if "V0" not in ORDER: own_wave.wait()
        settle(*list(owed))
        return

    rows = []
    for h in range(chunks):
        settle(("got", "z", h))
        rows.append(jnp.sum(landed[h], axis=0))
    block = jnp.concatenate(rows + [jnp.zeros((128 - chunks * height, 128), jnp.float32)], axis=0)
    turned = lax.dot_general(
        mixing, block, (((1,), (1,)), ((), ())), precision=lax.Precision.HIGHEST, preferred_element_type=jnp.float32
    )
    mixed[...] = turned.reshape(mixed.shape)

    @pl.loop(1, n)
    def _(j):
        to = (col + j) % n
        remote(mixed.at[to], final.at[col], f_send, f_recv, (row, to)).start()

    final[col] = mixed[col]
    wait(final.at[pl.ds(0, n - 1)], f_recv)
    out[...] = final[...].reshape(size, 128).T[: chunks * height]

    wait(final.at[pl.ds(0, n - 1)], f_send)
    settle(*list(owed))


def shards(env, wave, mpo):
    n = lax.axis_size("row")
    rows, depth = env.shape
    height = rows // CHUNKS
    wave4 = wave.reshape(X, 2, depth // (2 * X), wave.shape[1])
    f32, bf16 = jnp.float32, jnp.bfloat16
    dma = pltpu.SemaphoreType.DMA
    h = CHUNKS
    return pl.pallas_call(
        kernel,
        out_shape=jax.ShapeDtypeStruct((rows, 128), f32),
        in_specs=[
            pl.BlockSpec(memory_space=pltpu.HBM),
            pl.BlockSpec(memory_space=pltpu.HBM),
            pl.BlockSpec(memory_space=pltpu.HBM),
        ],
        out_specs=pl.BlockSpec(memory_space=pltpu.VMEM),
        scratch_shapes=[
            pltpu.VMEM((h, X, height, depth // X), f32),
            pltpu.VMEM((h, X, n // 2, height, 256), f32),
            pltpu.VMEM((2, 2, X, depth // (2 * X), 128), f32),
            pltpu.VMEM((X, depth // (2 * X), 512), bf16),
            pltpu.VMEM((X, depth // (2 * X), 512), bf16),
            pltpu.VMEM((h, 2, 2, n // 2, height, 128), f32),
            pltpu.VMEM((h, 2, n // 2, height, 128), f32),
            pltpu.VMEM((h, 2, n // 2, height, 128), f32),
            pltpu.VMEM((h, n, height, 128), f32),
            pltpu.VMEM((n, 8, 128), f32),
            pltpu.VMEM((n, 8, 128), f32),
            pltpu.VMEM(mpo.shape, f32),
            dma((h,)), dma((h,)), dma((h,)), dma((h,)), dma((X,)), dma((X,)), dma((2,)), dma((2,)), dma((h, 4)), dma((h, 4)),
            dma((h,)), dma((h,)), dma((h,)), dma((h,)), dma, dma, dma, dma,
        ],
        compiler_params=pltpu.CompilerParams(
            collective_id=0, has_side_effects=True, vmem_limit_bytes=40 * 1024 * 1024
        ),
    )(env, wave4, mpo)


def solution(mesh):
    in_specs = (P("row", "col"), P("row", "col"), P())
    out_specs = P("row", "col")
    return jax.shard_map(shards, mesh=mesh, in_specs=in_specs, out_specs=out_specs, check_vma=False)
```

```python
import itertools

import jax
import jax.numpy as jnp
from jax import lax
from jax.experimental import pallas as pl
from jax.experimental.pallas import tpu as pltpu
from jax.sharding import PartitionSpec as P

MESH = pl.DeviceIdType.MESH
HEIGHTS = (24, 16, 16, 8)
GATED = (1, 2)
ORDER = (
    "W0", "W1", "A0", "W2", "W3", "S0", "A1", "B0", "A2",
    "A3", "B1", "O0", "B2", "O1", "B3", "S1", "V0", "O2",
    "M0", "O3", "M1", "R0", "M2", "R1", "M3", "R2", "R3",
)
X, Z = 4, 8


def device(yh, yl, x, z, core):
    return (yl * Z + z, yh * 2 * X + x * 2 + core)


def wrap(i, n):
    return jnp.where(i >= n, i - n, i)


def split(value):
    high = value.astype(jnp.bfloat16)
    return high, (value - high.astype(jnp.float32)).astype(jnp.bfloat16)


def dot(a, b):
    return jnp.dot(a, b, preferred_element_type=jnp.float32)


def kernel(
    env, wave, mpo, out, spread, gathered, waves, wave_high, wave_low, part, other, summed, landed, mixed, final, table,
    a_send, a_recv, b_send, b_recv, w_send, w_recv, s_send, s_recv, g_send, g_recv, y_send, y_recv, z_send, z_recv,
    f_send, f_recv, w_local, t_local,
):
    row, col = lax.axis_index("row"), lax.axis_index("col")
    yl, yh = jnp.where(row >= Z, 1, 0), jnp.where(col >= 2 * X, 1, 0)
    z = row - yl * Z
    x, core = lax.div(col, 2) - yh * X, lax.rem(col, 2)
    zh, zl = lax.div(z, 2), lax.rem(z, 2)
    chunks = len(landed)
    n = landed[0].shape[0]
    heights = [ref.shape[1] for ref in landed]
    firsts = [sum(heights[:h]) for h in range(chunks)]

    def remote(src, dst, send, recv, to):
        return pltpu.make_async_remote_copy(
            src_ref=src, dst_ref=dst, send_sem=send, recv_sem=recv, device_id=to, device_id_type=MESH
        )

    def wait(ref, sem):
        pltpu.make_async_copy(ref, ref, sem).wait()

    right = device(yh, yl, wrap(x + 1, X), z, core)
    left = device(yh, yl, wrap(x + X - 1, X), z, core)
    opposite = device(yh, yl, wrap(x + 2, X), z, core)
    sibling = device(yh, yl, x, z, 1 - core)
    across = device(1 - yh, yl, x, z, core)

    barrier = pltpu.get_barrier_semaphore()

    def greet(to):
        pl.semaphore_signal(barrier, inc=1, device_id=to, device_id_type=MESH)

    for step in range(1, X):
        greet(device(yh, yl, wrap(x + step, X), z, core))
    greet(sibling)
    greet(across)
    source = yl * 2 * X + x * 2 + zl
    reducer = yh * 2 * X + x * 2 + zl

    @pl.loop(0, n // 2)
    def _(j):
        greet((2 * j + core, source))

    @pl.loop(0, n)
    def _(j):
        greet((j, reducer))

    @pl.loop(1, n)
    def _(j):
        greet((row, wrap(col + j, n)))

    own_table = pltpu.make_async_copy(mpo, table, t_local)
    own_table.start()
    own_wave = pltpu.make_async_copy(wave.at[:, yh], waves.at[yh, core], w_local)
    own_wave.start()

    own_table.wait()
    spins = mpo.shape[0]
    size = mixed.shape[0] * mixed.shape[1]
    rights = size // spins
    wide = lax.broadcasted_iota(jnp.int32, (size, spins), 0)
    pick_t = (wide // rights == lax.broadcasted_iota(jnp.int32, (size, spins), 1)).astype(jnp.float32)
    tall = lax.broadcasted_iota(jnp.int32, (spins, size), 1)
    pick_s = (tall % spins == lax.broadcasted_iota(jnp.int32, (spins, size), 0)).astype(jnp.float32)
    by_t = lax.dot_general(
        pick_t, table[...], (((1,), (1,)), ((), ())), precision=lax.Precision.HIGHEST,
        preferred_element_type=jnp.float32,
    )
    full = jnp.dot(by_t, pick_s, precision=lax.Precision.HIGHEST, preferred_element_type=jnp.float32)
    same = (
        lax.broadcasted_iota(jnp.int32, (size, size), 0) % rights
        == lax.broadcasted_iota(jnp.int32, (size, size), 1) // spins
    )
    mixing = jnp.where(same, full, 0.0)

    pl.semaphore_wait(barrier, (X - 1) + 2 + n // 2 + n + (n - 1))

    wide_k = spread[0].shape[2]

    def slices(h, to_x):
        return env.at[pl.ds(firsts[h], heights[h]), pl.ds(pl.multiple_of(to_x * wide_k, wide_k), wide_k)]

    owed = {}

    def settle(*keys):
        for key in keys:
            if key in owed:
                owed.pop(key)()

    def start(key, src, dst, send, recv, to, landing=None):
        remote(src, dst, send, recv, to).start()
        owed[("sent", *key)] = lambda: wait(src, send)
        owed[("got", *key)] = lambda: wait(dst if landing is None else landing, recv)

    def spread_out(h):
        settle(("sent", "a", h - 1))
        for step in range(1, X):
            to_x = wrap(x + step, X)
            to = device(yh, yl, to_x, z, core)
            remote(slices(h, to_x), spread[h].at[x], a_send.at[h], a_recv.at[h], to).start()
        pltpu.make_async_copy(slices(h, x), spread[h].at[x], a_recv.at[h]).start()
        owed["sent", "a", h] = lambda: wait(spread[h].at[pl.ds(0, X - 1)], a_send.at[h])
        owed["got", "a", h] = lambda: wait(spread[h], a_recv.at[h])

    def cross(p):
        dst = waves.at[yh, core, p]
        start(("w", p), wave.at[p, 1 - yh], dst, w_send.at[p], w_recv.at[p], across, waves.at[1 - yh, core, p])

    def share(i):
        if i == 0:
            src = wave.at[:, yh]
        else:
            src = waves.at[1 - yh, core]
            settle(*(("got", "w", p) for p in range(X)))
        q = yh if i == 0 else 1 - yh
        start(("s", i), src, waves.at[q, core], s_send.at[i], s_recv.at[i], sibling, waves.at[q, 1 - core])

    def wave_ready(_):
        own_wave.wait()
        settle(("got", "s", 0), ("got", "s", 1))
        for p in range(X):
            high, low = split(jnp.concatenate([waves[q // 2, q % 2, p] for q in range(4)], axis=1))
            wave_high[p] = high
            wave_low[p] = low

    def scatter(key, count, piece, send, recv, whole, may_be_here):
        @pl.loop(0, X)
        def _(i):
            for src, dst, to, here in piece(i):
                @pl.when(jnp.logical_not(here))
                def _():
                    remote(src, dst, send, recv, to).start()

                @pl.when(here)
                def _():
                    pltpu.make_async_copy(src, dst, recv).start()

        def sent():
            @pl.when(may_be_here)
            def _():
                wait(whole.at[pl.ds(0, count - 1)], send)

            @pl.when(jnp.logical_not(may_be_here))
            def _():
                wait(whole, send)

        owed[("sent", *key)] = sent
        owed[("got", *key)] = lambda: wait(whole, recv)

    def forward(h):
        settle(("got", "a", h))
        settle(("sent", "b", h - 1))

        def piece(i):
            from_x = wrap(zh + i, X)
            for to_yh in range(2):
                src = spread[h].at[from_x, :, pl.ds(to_yh * 256, 256)]
                here = (yl == yh) & (to_yh == yh) & (2 * from_x + core == z)
                yield src, gathered[h].at[x, yl * X + zh], device(to_yh, yh, x, 2 * from_x + core, zl), here

        scatter(("b", h), 2 * X, piece, b_send.at[h], b_recv.at[h], gathered[h].at[x], (yl == yh) & (zl == core))

    from_left, from_right, far = (wrap(x + s, X) for s in (3, 1, 2))

    def gather_own(h):
        settle(("got", "b", h))
        if h in GATED:
            settle(("sent", "g", h - 1, 0), ("sent", "g", h - 1, 1))
        own = gathered[h].at[x]
        start(("g", h, 0), own, own, g_send.at[h, 0], g_recv.at[h, 0], right, gathered[h].at[from_left])
        start(("g", h, 1), own, own, g_send.at[h, 1], g_recv.at[h, 1], left, gathered[h].at[from_right])
        start(("g", h, 2), own, own, g_send.at[h, 2], g_recv.at[h, 2], opposite, gathered[h].at[far])

    def multiply(h):
        settle(*(("got", "g", h, i) for i in range(3)))
        total = None
        height = heights[h]
        size = n // 2 * height
        for p in range(X):
            high, low = split(gathered[h][p].reshape(size, 256))
            both = dot(jnp.concatenate([high, low], axis=0), wave_high[p])
            term = both[:size] + both[size:] + dot(high, wave_low[p])
            total = term if total is None else total + term
        for q in range(4):
            part[h][q // 2, q % 2] = total[:, q * 128 : (q + 1) * 128].reshape(n // 2, height, 128)
        start(("y", h), part[h].at[1 - yh], other[h], y_send.at[h], y_recv.at[h], across)

    def reduce(h):
        settle(("got", "y", h))
        summed[h][...] = part[h][yh] + other[h][...]

        def piece(i):
            zz = wrap(zh + i, X)
            for to_yl, to_core in itertools.product(range(2), repeat=2):
                src = summed[h].at[to_core, to_yl * X + zz]
                here = (2 * zz + core == z) & (to_yl == yl) & (to_core == core)
                yield src, landed[h].at[row], device(yh, to_yl, x, 2 * zz + core, to_core), here

        scatter(("z", h), n, piece, z_send.at[h], z_recv.at[h], landed[h], zl == core)

    steps = dict(A=spread_out, B=forward, O=gather_own, M=multiply, R=reduce, W=cross, S=share, V=wave_ready)
    for step in ORDER:
        steps[step[0]](int(step[1:]))

    rows = []
    for h in range(chunks):
        settle(("got", "z", h))
        rows.append(jnp.sum(landed[h][...], axis=0))
    block = jnp.concatenate(rows + [jnp.zeros((128 - sum(heights), 128), jnp.float32)], axis=0)
    turned = lax.dot_general(
        mixing, block, (((1,), (1,)), ((), ())), precision=lax.Precision.HIGHEST, preferred_element_type=jnp.float32
    )
    mixed[...] = turned.reshape(mixed.shape)

    @pl.loop(1, n)
    def _(j):
        to = wrap(col + j, n)
        remote(mixed.at[to], final.at[col], f_send, f_recv, (row, to)).start()

    final[col] = mixed[col]
    wait(final.at[pl.ds(0, n - 1)], f_recv)
    out[...] = final[...].reshape(size, 128).T[: sum(heights)]

    wait(final.at[pl.ds(0, n - 1)], f_send)
    settle(*list(owed))


def shards(env, wave, mpo):
    n = lax.axis_size("row")
    rows, depth = env.shape
    wave4 = wave.reshape(X, 2, depth // (2 * X), wave.shape[1])
    f32, bf16 = jnp.float32, jnp.bfloat16
    dma = pltpu.SemaphoreType.DMA
    h = len(HEIGHTS)
    return pl.pallas_call(
        kernel,
        out_shape=jax.ShapeDtypeStruct((rows, 128), f32),
        in_specs=[
            pl.BlockSpec(memory_space=pltpu.HBM),
            pl.BlockSpec(memory_space=pltpu.HBM),
            pl.BlockSpec(memory_space=pltpu.HBM),
        ],
        out_specs=pl.BlockSpec(memory_space=pltpu.VMEM),
        scratch_shapes=[
            [pltpu.VMEM((X, height, depth // X), f32) for height in HEIGHTS],
            [pltpu.VMEM((X, n // 2, height, 256), f32) for height in HEIGHTS],
            pltpu.VMEM((2, 2, X, depth // (2 * X), 128), f32),
            pltpu.VMEM((X, depth // (2 * X), 512), bf16),
            pltpu.VMEM((X, depth // (2 * X), 512), bf16),
            [pltpu.VMEM((2, 2, n // 2, height, 128), f32) for height in HEIGHTS],
            [pltpu.VMEM((2, n // 2, height, 128), f32) for height in HEIGHTS],
            [pltpu.VMEM((2, n // 2, height, 128), f32) for height in HEIGHTS],
            [pltpu.VMEM((n, height, 128), f32) for height in HEIGHTS],
            pltpu.VMEM((n, 8, 128), f32),
            pltpu.VMEM((n, 8, 128), f32),
            pltpu.VMEM(mpo.shape, f32),
            dma((h,)), dma((h,)), dma((h,)), dma((h,)), dma((X,)), dma((X,)), dma((2,)), dma((2,)), dma((h, 3)), dma((h, 3)),
            dma((h,)), dma((h,)), dma((h,)), dma((h,)), dma, dma, dma, dma,
        ],
        compiler_params=pltpu.CompilerParams(
            collective_id=0, has_side_effects=True, vmem_limit_bytes=40 * 1024 * 1024
        ),
    )(env, wave4, mpo)


def solution(mesh):
    in_specs = (P("row", "col"), P("row", "col"), P())
    out_specs = P("row", "col")
    return jax.shard_map(shards, mesh=mesh, in_specs=in_specs, out_specs=out_specs, check_vma=False)
```

```python
import itertools

import jax
import jax.numpy as jnp
from jax import lax
from jax.experimental import pallas as pl
from jax.experimental.pallas import tpu as pltpu
from jax.sharding import PartitionSpec as P

MESH = pl.DeviceIdType.MESH
HEIGHTS = (24, 16, 16, 8)
GATED = (1, 2)
ORDER = (
    "W0", "W1", "A0", "W2", "W3", "S0", "A1", "B0", "A2",
    "A3", "B1", "O0", "B2", "O1", "B3", "S1", "V0", "O2",
    "M0", "O3", "M1", "M2", "R0", "M3", "R1", "R2", "R3",
)
X, Z = 4, 8


def device(yh, yl, x, z, core):
    return (yl * Z + z, yh * 2 * X + x * 2 + core)


def wrap(i, n):
    return jnp.where(i >= n, i - n, i)


def split(value):
    high = value.astype(jnp.bfloat16)
    return high, (value - high.astype(jnp.float32)).astype(jnp.bfloat16)


def dot(a, b):
    return jnp.dot(a, b, preferred_element_type=jnp.float32)


def kernel(
    env, wave, mpo, out, spread, gathered, waves, wave_high, wave_low, part, other, summed, landed, mixed, final, table,
    a_send, a_recv, b_send, b_recv, w_send, w_recv, s_send, s_recv, g_send, g_recv, y_send, y_recv, z_send, z_recv,
    f_send, f_recv, w_local, t_local,
):
    row, col = lax.axis_index("row"), lax.axis_index("col")
    yl, yh = jnp.where(row >= Z, 1, 0), jnp.where(col >= 2 * X, 1, 0)
    z = row - yl * Z
    x, core = lax.div(col, 2) - yh * X, lax.rem(col, 2)
    zh, zl = lax.div(z, 2), lax.rem(z, 2)
    chunks = len(landed)
    n = landed[0].shape[0]
    heights = [ref.shape[1] for ref in landed]
    firsts = [sum(heights[:h]) for h in range(chunks)]

    def remote(src, dst, send, recv, to):
        return pltpu.make_async_remote_copy(
            src_ref=src, dst_ref=dst, send_sem=send, recv_sem=recv, device_id=to, device_id_type=MESH
        )

    def wait(ref, sem):
        pltpu.make_async_copy(ref, ref, sem).wait()

    right = device(yh, yl, wrap(x + 1, X), z, core)
    left = device(yh, yl, wrap(x + X - 1, X), z, core)
    opposite = device(yh, yl, wrap(x + 2, X), z, core)
    sibling = device(yh, yl, x, z, 1 - core)
    across = device(1 - yh, yl, x, z, core)

    barrier = pltpu.get_barrier_semaphore()

    def greet(to):
        pl.semaphore_signal(barrier, inc=1, device_id=to, device_id_type=MESH)

    for step in range(1, X):
        greet(device(yh, yl, wrap(x + step, X), z, core))
    greet(sibling)
    greet(across)
    source = yl * 2 * X + x * 2 + zl
    reducer = yh * 2 * X + x * 2 + zl

    @pl.loop(0, n // 2)
    def _(j):
        greet((2 * j + core, source))

    @pl.loop(0, n)
    def _(j):
        greet((j, reducer))

    @pl.loop(1, n)
    def _(j):
        greet((row, wrap(col + j, n)))

    own_table = pltpu.make_async_copy(mpo, table, t_local)
    own_table.start()
    own_wave = pltpu.make_async_copy(wave.at[:, yh], waves.at[yh, core], w_local)
    own_wave.start()

    own_table.wait()
    spins = mpo.shape[0]
    size = mixed.shape[0] * mixed.shape[1]
    rights = size // spins
    wide = lax.broadcasted_iota(jnp.int32, (size, spins), 0)
    pick_t = (wide // rights == lax.broadcasted_iota(jnp.int32, (size, spins), 1)).astype(jnp.float32)
    tall = lax.broadcasted_iota(jnp.int32, (spins, size), 1)
    pick_s = (tall % spins == lax.broadcasted_iota(jnp.int32, (spins, size), 0)).astype(jnp.float32)
    by_t = lax.dot_general(
        pick_t, table[...], (((1,), (1,)), ((), ())), precision=lax.Precision.HIGHEST,
        preferred_element_type=jnp.float32,
    )
    full = jnp.dot(by_t, pick_s, precision=lax.Precision.HIGHEST, preferred_element_type=jnp.float32)
    same = (
        lax.broadcasted_iota(jnp.int32, (size, size), 0) % rights
        == lax.broadcasted_iota(jnp.int32, (size, size), 1) // spins
    )
    mixing = jnp.where(same, full, 0.0)

    pl.semaphore_wait(barrier, (X - 1) + 2 + n // 2 + n + (n - 1))

    wide_k = spread[0].shape[2]

    def slices(h, to_x):
        return env.at[pl.ds(firsts[h], heights[h]), pl.ds(pl.multiple_of(to_x * wide_k, wide_k), wide_k)]

    owed = {}

    def settle(*keys):
        for key in keys:
            if key in owed:
                owed.pop(key)()

    def start(key, src, dst, send, recv, to, landing=None):
        remote(src, dst, send, recv, to).start()
        owed[("sent", *key)] = lambda: wait(src, send)
        owed[("got", *key)] = lambda: wait(dst if landing is None else landing, recv)

    def spread_out(h):
        settle(("sent", "a", h - 1))
        for step in range(1, X):
            to_x = wrap(x + step, X)
            to = device(yh, yl, to_x, z, core)
            remote(slices(h, to_x), spread[h].at[x], a_send.at[h], a_recv.at[h], to).start()
        pltpu.make_async_copy(slices(h, x), spread[h].at[x], a_recv.at[h]).start()
        owed["sent", "a", h] = lambda: wait(spread[h].at[pl.ds(0, X - 1)], a_send.at[h])
        owed["got", "a", h] = lambda: wait(spread[h], a_recv.at[h])

    def cross(p):
        dst = waves.at[yh, core, p]
        start(("w", p), wave.at[p, 1 - yh], dst, w_send.at[p], w_recv.at[p], across, waves.at[1 - yh, core, p])

    def share(i):
        if i == 0:
            src = wave.at[:, yh]
        else:
            src = waves.at[1 - yh, core]
            settle(*(("got", "w", p) for p in range(X)))
        q = yh if i == 0 else 1 - yh
        start(("s", i), src, waves.at[q, core], s_send.at[i], s_recv.at[i], sibling, waves.at[q, 1 - core])

    def wave_ready(_):
        own_wave.wait()
        settle(("got", "s", 0), ("got", "s", 1))
        for p in range(X):
            high, low = split(jnp.concatenate([waves[q // 2, q % 2, p] for q in range(4)], axis=1))
            wave_high[p] = high
            wave_low[p] = low

    def scatter(key, count, piece, send, recv, whole, may_be_here):
        @pl.loop(0, X)
        def _(i):
            for src, dst, to, here in piece(i):
                @pl.when(jnp.logical_not(here))
                def _():
                    remote(src, dst, send, recv, to).start()

                @pl.when(here)
                def _():
                    pltpu.make_async_copy(src, dst, recv).start()

        def sent():
            @pl.when(may_be_here)
            def _():
                wait(whole.at[pl.ds(0, count - 1)], send)

            @pl.when(jnp.logical_not(may_be_here))
            def _():
                wait(whole, send)

        owed[("sent", *key)] = sent
        owed[("got", *key)] = lambda: wait(whole, recv)

    def forward(h):
        settle(("got", "a", h))
        settle(("sent", "b", h - 1))

        def piece(i):
            from_x = wrap(zh + i, X)
            for to_yh in range(2):
                src = spread[h].at[from_x, :, pl.ds(to_yh * 256, 256)]
                here = (yl == yh) & (to_yh == yh) & (2 * from_x + core == z)
                yield src, gathered[h].at[x, yl * X + zh], device(to_yh, yh, x, 2 * from_x + core, zl), here

        scatter(("b", h), 2 * X, piece, b_send.at[h], b_recv.at[h], gathered[h].at[x], (yl == yh) & (zl == core))

    from_left, from_right, far = (wrap(x + s, X) for s in (3, 1, 2))

    def gather_own(h):
        settle(("got", "b", h))
        if h in GATED:
            settle(("sent", "g", h - 1, 0), ("sent", "g", h - 1, 1))
        own = gathered[h].at[x]
        start(("g", h, 0), own, own, g_send.at[h, 0], g_recv.at[h, 0], right, gathered[h].at[from_left])
        start(("g", h, 1), own, own, g_send.at[h, 1], g_recv.at[h, 1], left, gathered[h].at[from_right])
        start(("g", h, 2), own, own, g_send.at[h, 2], g_recv.at[h, 2], opposite, gathered[h].at[far])

    def multiply(h):
        settle(*(("got", "g", h, i) for i in range(3)))
        total = None
        height = heights[h]
        size = n // 2 * height
        for p in range(X):
            high, low = split(gathered[h][p].reshape(size, 256))
            both = dot(jnp.concatenate([high, low], axis=0), wave_high[p])
            term = both[:size] + both[size:] + dot(high, wave_low[p])
            total = term if total is None else total + term
        for q in range(4):
            part[h][q // 2, q % 2] = total[:, q * 128 : (q + 1) * 128].reshape(n // 2, height, 128)
        start(("y", h), part[h].at[1 - yh], other[h], y_send.at[h], y_recv.at[h], across)

    def reduce(h):
        settle(("got", "y", h))
        summed[h][...] = part[h][yh] + other[h][...]

        def piece(i):
            zz = wrap(zh + i, X)
            for to_yl, to_core in itertools.product(range(2), repeat=2):
                src = summed[h].at[to_core, to_yl * X + zz]
                here = (2 * zz + core == z) & (to_yl == yl) & (to_core == core)
                yield src, landed[h].at[row], device(yh, to_yl, x, 2 * zz + core, to_core), here

        scatter(("z", h), n, piece, z_send.at[h], z_recv.at[h], landed[h], zl == core)

    steps = dict(A=spread_out, B=forward, O=gather_own, M=multiply, R=reduce, W=cross, S=share, V=wave_ready)
    for step in ORDER:
        steps[step[0]](int(step[1:]))

    rows = []
    for h in range(chunks):
        settle(("got", "z", h))
        rows.append(jnp.sum(landed[h][...], axis=0))
    block = jnp.concatenate(rows + [jnp.zeros((128 - sum(heights), 128), jnp.float32)], axis=0)
    turned = lax.dot_general(
        mixing, block, (((1,), (1,)), ((), ())), precision=lax.Precision.HIGHEST, preferred_element_type=jnp.float32
    )
    mixed[...] = turned.reshape(mixed.shape)

    @pl.loop(1, n)
    def _(j):
        to = wrap(col + j, n)
        remote(mixed.at[to], final.at[col], f_send, f_recv, (row, to)).start()

    final[col] = mixed[col]
    wait(final.at[pl.ds(0, n - 1)], f_recv)
    out[...] = final[...].reshape(size, 128).T[: sum(heights)]

    wait(final.at[pl.ds(0, n - 1)], f_send)
    settle(*list(owed))


def shards(env, wave, mpo):
    n = lax.axis_size("row")
    rows, depth = env.shape
    wave4 = wave.reshape(X, 2, depth // (2 * X), wave.shape[1])
    f32, bf16 = jnp.float32, jnp.bfloat16
    dma = pltpu.SemaphoreType.DMA
    h = len(HEIGHTS)
    return pl.pallas_call(
        kernel,
        out_shape=jax.ShapeDtypeStruct((rows, 128), f32),
        in_specs=[
            pl.BlockSpec(memory_space=pltpu.HBM),
            pl.BlockSpec(memory_space=pltpu.HBM),
            pl.BlockSpec(memory_space=pltpu.HBM),
        ],
        out_specs=pl.BlockSpec(memory_space=pltpu.VMEM),
        scratch_shapes=[
            [pltpu.VMEM((X, height, depth // X), f32) for height in HEIGHTS],
            [pltpu.VMEM((X, n // 2, height, 256), f32) for height in HEIGHTS],
            pltpu.VMEM((2, 2, X, depth // (2 * X), 128), f32),
            pltpu.VMEM((X, depth // (2 * X), 512), bf16),
            pltpu.VMEM((X, depth // (2 * X), 512), bf16),
            [pltpu.VMEM((2, 2, n // 2, height, 128), f32) for height in HEIGHTS],
            [pltpu.VMEM((2, n // 2, height, 128), f32) for height in HEIGHTS],
            [pltpu.VMEM((2, n // 2, height, 128), f32) for height in HEIGHTS],
            [pltpu.VMEM((n, height, 128), f32) for height in HEIGHTS],
            pltpu.VMEM((n, 8, 128), f32),
            pltpu.VMEM((n, 8, 128), f32),
            pltpu.VMEM(mpo.shape, f32),
            dma((h,)), dma((h,)), dma((h,)), dma((h,)), dma((X,)), dma((X,)), dma((2,)), dma((2,)), dma((h, 3)), dma((h, 3)),
            dma((h,)), dma((h,)), dma((h,)), dma((h,)), dma, dma, dma, dma,
        ],
        compiler_params=pltpu.CompilerParams(
            collective_id=0, has_side_effects=True, vmem_limit_bytes=40 * 1024 * 1024
        ),
    )(env, wave4, mpo)


def solution(mesh):
    in_specs = (P("row", "col"), P("row", "col"), P())
    out_specs = P("row", "col")
    return jax.shard_map(shards, mesh=mesh, in_specs=in_specs, out_specs=out_specs, check_vma=False)
```

```python
import itertools

import jax
import jax.numpy as jnp
from jax import lax
from jax.experimental import pallas as pl
from jax.experimental.pallas import tpu as pltpu
from jax.sharding import PartitionSpec as P

MESH = pl.DeviceIdType.MESH
HEIGHTS = (24, 16, 16, 8)
GATED = (1, 2)
ORDER = (
    "W0", "W1", "A0", "W2", "W3", "S0", "A1", "B0", "A2",
    "A3", "B1", "O0", "B2", "O1", "B3", "S1", "V0", "O2",
    "M0", "O3", "M1", "M2", "R0", "M3", "R1", "R2", "R3",
)
X, Z = 4, 8


def device(yh, yl, x, z, core):
    return (yl * Z + z, yh * 2 * X + x * 2 + core)


def wrap(i, n):
    return jnp.where(i >= n, i - n, i)


def split(value):
    high = value.astype(jnp.bfloat16)
    return high, (value - high.astype(jnp.float32)).astype(jnp.bfloat16)


def dot(a, b):
    return jnp.dot(a, b, preferred_element_type=jnp.float32)


def kernel(
    env, wave, mpo, out, spread, gathered, waves, wave_high, wave_low, part, other, summed, landed, mixed, final, table,
    a_send, a_recv, b_send, b_recv, w_send, w_recv, s_send, s_recv, g_send, g_recv, y_send, y_recv, z_send, z_recv,
    f_send, f_recv, w_local, t_local,
):
    row, col = lax.axis_index("row"), lax.axis_index("col")
    yl, yh = jnp.where(row >= Z, 1, 0), jnp.where(col >= 2 * X, 1, 0)
    z = row - yl * Z
    x, core = lax.div(col, 2) - yh * X, lax.rem(col, 2)
    zh, zl = lax.div(z, 2), lax.rem(z, 2)
    chunks = len(landed)
    n = landed[0].shape[0]
    heights = [ref.shape[1] for ref in landed]
    firsts = [sum(heights[:h]) for h in range(chunks)]

    def remote(src, dst, send, recv, to):
        return pltpu.make_async_remote_copy(
            src_ref=src, dst_ref=dst, send_sem=send, recv_sem=recv, device_id=to, device_id_type=MESH
        )

    def wait(ref, sem):
        pltpu.make_async_copy(ref, ref, sem).wait()

    right = device(yh, yl, wrap(x + 1, X), z, core)
    left = device(yh, yl, wrap(x + X - 1, X), z, core)
    opposite = device(yh, yl, wrap(x + 2, X), z, core)
    sibling = device(yh, yl, x, z, 1 - core)
    across = device(1 - yh, yl, x, z, core)

    barrier = pltpu.get_barrier_semaphore()

    def greet(to):
        pl.semaphore_signal(barrier, inc=1, device_id=to, device_id_type=MESH)

    for step in range(1, X):
        greet(device(yh, yl, wrap(x + step, X), z, core))
    greet(sibling)
    greet(across)
    source = yl * 2 * X + x * 2 + zl
    reducer = yh * 2 * X + x * 2 + zl

    @pl.loop(0, n // 2)
    def _(j):
        greet((2 * j + core, source))

    @pl.loop(0, n)
    def _(j):
        greet((j, reducer))

    @pl.loop(1, n)
    def _(j):
        greet((row, wrap(col + j, n)))

    own_table = pltpu.make_async_copy(mpo, table, t_local)
    own_table.start()
    own_wave = pltpu.make_async_copy(wave.at[:, yh], waves.at[yh, core], w_local)
    own_wave.start()

    pl.semaphore_wait(barrier, (X - 1) + 2 + n // 2 + n + (n - 1))

    wide_k = spread[0].shape[2]

    def slices(h, to_x):
        return env.at[pl.ds(firsts[h], heights[h]), pl.ds(pl.multiple_of(to_x * wide_k, wide_k), wide_k)]

    owed = {}

    def settle(*keys):
        for key in keys:
            if key in owed:
                owed.pop(key)()

    def start(key, src, dst, send, recv, to, landing=None):
        remote(src, dst, send, recv, to).start()
        owed[("sent", *key)] = lambda: wait(src, send)
        owed[("got", *key)] = lambda: wait(dst if landing is None else landing, recv)

    def spread_out(h):
        settle(("sent", "a", h - 1))
        for step in range(1, X):
            to_x = wrap(x + step, X)
            to = device(yh, yl, to_x, z, core)
            remote(slices(h, to_x), spread[h].at[x], a_send.at[h], a_recv.at[h], to).start()
        pltpu.make_async_copy(slices(h, x), spread[h].at[x], a_recv.at[h]).start()
        owed["sent", "a", h] = lambda: wait(spread[h].at[pl.ds(0, X - 1)], a_send.at[h])
        owed["got", "a", h] = lambda: wait(spread[h], a_recv.at[h])

    def cross(p):
        dst = waves.at[yh, core, p]
        start(("w", p), wave.at[p, 1 - yh], dst, w_send.at[p], w_recv.at[p], across, waves.at[1 - yh, core, p])

    def share(i):
        if i == 0:
            src = wave.at[:, yh]
        else:
            src = waves.at[1 - yh, core]
            settle(*(("got", "w", p) for p in range(X)))
        q = yh if i == 0 else 1 - yh
        start(("s", i), src, waves.at[q, core], s_send.at[i], s_recv.at[i], sibling, waves.at[q, 1 - core])

    def wave_ready(_):
        own_wave.wait()
        settle(("got", "s", 0), ("got", "s", 1))
        for p in range(X):
            high, low = split(jnp.concatenate([waves[q // 2, q % 2, p] for q in range(4)], axis=1))
            wave_high[p] = high
            wave_low[p] = low

    def scatter(key, count, piece, send, recv, whole, may_be_here):
        @pl.loop(0, X)
        def _(i):
            for src, dst, to, here in piece(i):
                @pl.when(jnp.logical_not(here))
                def _():
                    remote(src, dst, send, recv, to).start()

                @pl.when(here)
                def _():
                    pltpu.make_async_copy(src, dst, recv).start()

        def sent():
            @pl.when(may_be_here)
            def _():
                wait(whole.at[pl.ds(0, count - 1)], send)

            @pl.when(jnp.logical_not(may_be_here))
            def _():
                wait(whole, send)

        owed[("sent", *key)] = sent
        owed[("got", *key)] = lambda: wait(whole, recv)

    def forward(h):
        settle(("got", "a", h))
        settle(("sent", "b", h - 1))

        def piece(i):
            from_x = wrap(zh + i, X)
            for to_yh in range(2):
                src = spread[h].at[from_x, :, pl.ds(to_yh * 256, 256)]
                here = (yl == yh) & (to_yh == yh) & (2 * from_x + core == z)
                yield src, gathered[h].at[x, yl * X + zh], device(to_yh, yh, x, 2 * from_x + core, zl), here

        scatter(("b", h), 2 * X, piece, b_send.at[h], b_recv.at[h], gathered[h].at[x], (yl == yh) & (zl == core))

    from_left, from_right, far = (wrap(x + s, X) for s in (3, 1, 2))

    def gather_own(h):
        settle(("got", "b", h))
        if h in GATED:
            settle(("sent", "g", h - 1, 0), ("sent", "g", h - 1, 1))
        own = gathered[h].at[x]
        start(("g", h, 0), own, own, g_send.at[h, 0], g_recv.at[h, 0], right, gathered[h].at[from_left])
        start(("g", h, 1), own, own, g_send.at[h, 1], g_recv.at[h, 1], left, gathered[h].at[from_right])
        start(("g", h, 2), own, own, g_send.at[h, 2], g_recv.at[h, 2], opposite, gathered[h].at[far])

    def multiply(h):
        settle(*(("got", "g", h, i) for i in range(3)))
        total = None
        height = heights[h]
        size = n // 2 * height
        for p in range(X):
            high, low = split(gathered[h][p].reshape(size, 256))
            both = dot(jnp.concatenate([high, low], axis=0), wave_high[p])
            term = both[:size] + both[size:] + dot(high, wave_low[p])
            total = term if total is None else total + term
        for q in range(4):
            part[h][q // 2, q % 2] = total[:, q * 128 : (q + 1) * 128].reshape(n // 2, height, 128)
        start(("y", h), part[h].at[1 - yh], other[h], y_send.at[h], y_recv.at[h], across)

    def reduce(h):
        settle(("got", "y", h))
        summed[h][...] = part[h][yh] + other[h][...]

        def piece(i):
            zz = wrap(zh + i, X)
            for to_yl, to_core in itertools.product(range(2), repeat=2):
                src = summed[h].at[to_core, to_yl * X + zz]
                here = (2 * zz + core == z) & (to_yl == yl) & (to_core == core)
                yield src, landed[h].at[row], device(yh, to_yl, x, 2 * zz + core, to_core), here

        scatter(("z", h), n, piece, z_send.at[h], z_recv.at[h], landed[h], zl == core)

    steps = dict(A=spread_out, B=forward, O=gather_own, M=multiply, R=reduce, W=cross, S=share, V=wave_ready)
    for step in ORDER:
        steps[step[0]](int(step[1:]))

    own_table.wait()
    spins = mpo.shape[0]
    size = mixed.shape[0] * mixed.shape[1]
    rights = size // spins
    wide = lax.broadcasted_iota(jnp.int32, (size, spins), 0)
    pick_t = (wide // rights == lax.broadcasted_iota(jnp.int32, (size, spins), 1)).astype(jnp.float32)
    tall = lax.broadcasted_iota(jnp.int32, (spins, size), 1)
    pick_s = (tall % spins == lax.broadcasted_iota(jnp.int32, (spins, size), 0)).astype(jnp.float32)
    by_t = lax.dot_general(
        pick_t, table[...], (((1,), (1,)), ((), ())), precision=lax.Precision.HIGHEST,
        preferred_element_type=jnp.float32,
    )
    full = jnp.dot(by_t, pick_s, precision=lax.Precision.HIGHEST, preferred_element_type=jnp.float32)
    same = (
        lax.broadcasted_iota(jnp.int32, (size, size), 0) % rights
        == lax.broadcasted_iota(jnp.int32, (size, size), 1) // spins
    )
    mixing = jnp.where(same, full, 0.0)

    rows = []
    for h in range(chunks):
        settle(("got", "z", h))
        rows.append(jnp.sum(landed[h][...], axis=0))
    block = jnp.concatenate(rows + [jnp.zeros((128 - sum(heights), 128), jnp.float32)], axis=0)
    turned = lax.dot_general(
        mixing, block, (((1,), (1,)), ((), ())), precision=lax.Precision.HIGHEST, preferred_element_type=jnp.float32
    )
    mixed[...] = turned.reshape(mixed.shape)

    @pl.loop(1, n)
    def _(j):
        to = wrap(col + j, n)
        remote(mixed.at[to], final.at[col], f_send, f_recv, (row, to)).start()

    final[col] = mixed[col]
    wait(final.at[pl.ds(0, n - 1)], f_recv)
    out[...] = final[...].reshape(size, 128).T[: sum(heights)]

    wait(final.at[pl.ds(0, n - 1)], f_send)
    settle(*list(owed))


def shards(env, wave, mpo):
    n = lax.axis_size("row")
    rows, depth = env.shape
    wave4 = wave.reshape(X, 2, depth // (2 * X), wave.shape[1])
    f32, bf16 = jnp.float32, jnp.bfloat16
    dma = pltpu.SemaphoreType.DMA
    h = len(HEIGHTS)
    return pl.pallas_call(
        kernel,
        out_shape=jax.ShapeDtypeStruct((rows, 128), f32),
        in_specs=[
            pl.BlockSpec(memory_space=pltpu.HBM),
            pl.BlockSpec(memory_space=pltpu.HBM),
            pl.BlockSpec(memory_space=pltpu.HBM),
        ],
        out_specs=pl.BlockSpec(memory_space=pltpu.VMEM),
        scratch_shapes=[
            [pltpu.VMEM((X, height, depth // X), f32) for height in HEIGHTS],
            [pltpu.VMEM((X, n // 2, height, 256), f32) for height in HEIGHTS],
            pltpu.VMEM((2, 2, X, depth // (2 * X), 128), f32),
            pltpu.VMEM((X, depth // (2 * X), 512), bf16),
            pltpu.VMEM((X, depth // (2 * X), 512), bf16),
            [pltpu.VMEM((2, 2, n // 2, height, 128), f32) for height in HEIGHTS],
            [pltpu.VMEM((2, n // 2, height, 128), f32) for height in HEIGHTS],
            [pltpu.VMEM((2, n // 2, height, 128), f32) for height in HEIGHTS],
            [pltpu.VMEM((n, height, 128), f32) for height in HEIGHTS],
            pltpu.VMEM((n, 8, 128), f32),
            pltpu.VMEM((n, 8, 128), f32),
            pltpu.VMEM(mpo.shape, f32),
            dma((h,)), dma((h,)), dma((h,)), dma((h,)), dma((X,)), dma((X,)), dma((2,)), dma((2,)), dma((h, 3)), dma((h, 3)),
            dma((h,)), dma((h,)), dma((h,)), dma((h,)), dma, dma, dma, dma,
        ],
        compiler_params=pltpu.CompilerParams(
            collective_id=0, has_side_effects=True, vmem_limit_bytes=40 * 1024 * 1024
        ),
    )(env, wave4, mpo)


def solution(mesh):
    in_specs = (P("row", "col"), P("row", "col"), P())
    out_specs = P("row", "col")
    return jax.shard_map(shards, mesh=mesh, in_specs=in_specs, out_specs=out_specs, check_vma=False)
```
